32 devices in a mesh: parts: 2 (over y), req: 8 (over z, x), tp: 2 (over core).
Axes of the slice: x: 2, y: 2, z: 4, core: 2. Of those that a mesh axis runs over, the one named last changes fastest.
Arguments:
- counts: int32 [16], P('parts'), parts along dimension 0, may hold values from 1 to 2, as said below
- move_plan: int32 [32], P('parts'), parts along dimension 0, may hold values from 0 to 15, as said below
- ssm_state: float32 [32, 128, 4096], P(('parts', 'req'), 'tp'), parts along dimension 0, may hold values from -6 to 6
- conv_x_state: bfloat16 [32, 3, 8192], P(('parts', 'req'), None, 'tp'), parts along dimension 0, may hold values from -6 to 6
- conv_bc_state: bfloat16 [32, 3, 4, 128], P(('parts', 'req'), None, 'tp'), parts along dimension 0, may hold values from -6 to 6
- x_in: bfloat16 [32, 4, 8192], P(('parts', 'req'), None, 'tp'), parts along dimension 0, may hold values from -6 to 6
- bc_in: bfloat16 [32, 4, 4, 128], P(('parts', 'req'), None, 'tp'), parts along dimension 0, may hold values from -6 to 6
- z_in: bfloat16 [32, 4, 8192], P(('parts', 'req'), None, 'tp'), parts along dimension 0, may hold values from -6 to 6
- dt_in: float32 [32, 4, 128], P(('parts', 'req'), None, 'tp'), parts along dimension 0, may hold values from -1.5 to 1.5
- conv_w_x: float32 [4, 8192], P(None, 'tp'), may hold values from -3 to 3
- conv_b_x: float32 [8192], P('tp'), may hold values from -3 to 3
- conv_w_bc: float32 [4, 4, 128], P(None, 'tp'), may hold values from -3 to 3
- conv_b_bc: float32 [4, 128], P('tp'), may hold values from -3 to 3
- dt_bias: float32 [128], P('tp'), may hold values from -4 to -1
- a_log: float32 [128], P('tp'), may hold values from -2.5 to -0.5
- d_skip: float32 [128], P('tp'), may hold values from 0.3 to 1.5
- norm_w: float32 [8192], P('tp'), may hold values from 0.1 to 1.9
Outputs:
- y_out: bfloat16 [32, 4, 8192], P(('parts', 'req'), None, 'tp'), parts along dimension 0
- new_ssm: float32 [32, 128, 4096], P(('parts', 'req'), 'tp'), parts along dimension 0
- new_conv_x: bfloat16 [32, 3, 8192], P(('parts', 'req'), None, 'tp'), parts along dimension 0
- new_conv_bc: bfloat16 [32, 3, 4, 128], P(('parts', 'req'), None, 'tp'), parts along dimension 0
The draws below stay inside these ranges and needn't reach their ends.
There are 2 independent parts, one for each index of `parts`. The reference program is written for one: setup_inputs(seed, part) draws one part's arguments, and reference() takes and returns one part's arrays. A program takes and returns all parts, laid end to end along the dimension named above; an argument that names none is the same for every part. Nothing has to cross between parts.
Inputs may be any that keep to these rules, and one draw needn't show every extreme that they name: `counts`: at least 1; every draw has owners with 2 live requests. `move_plan`: A destination slot is owner times 2 plus a local slot. Entries of slots that are not live are meaningless. Live requests have distinct destinations. An owner sends at most 1 live requests to other owners and receives at most 1 from other owners, and keeps at most 1 of its own; both bounds are reached in every draw, and some owner has all 2 destination slots taken.
All inputs are finite; a program needn't handle non-finite values.
Results may differ from the reference program's by a relative error of at most 0.001.
Values may be sent and summed in bfloat16 or wider, within the bound.
A program may use at most 128 MiB of HBM per device.

```python
import jax
import jax.numpy as jnp
from jax import lax

H = 128
P_SIZE = 64
N = 64
G = 4
CAP = 2
STEPS = 4
REQS = 16
CAPS = 16
N_REQ = 8


def plan_draw(key):
    base = jax.random.fold_in(key, 11)
    keys = jax.random.split(base, 6)
    order = jax.random.permutation(keys[0], N_REQ).astype(jnp.int32)
    following = jnp.zeros((N_REQ,), jnp.int32).at[order].set(jnp.roll(order, -1))
    counts = 1 + jax.random.randint(keys[1], (N_REQ,), 0, 2)
    counts = counts.at[order[0]].set(2).at[order[1]].set(2)
    leaves = jnp.where(counts == 2, 1, jax.random.randint(keys[2], (N_REQ,), 0, 2))
    leaving_slot = jnp.where(counts == 2, jax.random.randint(keys[3], (N_REQ,), 0, 2), 0)
    side = jax.random.randint(keys[4], (N_REQ,), 0, 2)
    owners = jnp.arange(N_REQ, dtype=jnp.int32)
    junk = jax.random.randint(keys[5], (N_REQ, 2), 0, N_REQ * CAP)
    moved_dest = following * CAP + jnp.take(side, following)
    stay_dest = owners * CAP + 1 - side
    columns = []
    for slot in range(2):
        live = slot < counts
        moving = live & (leaves == 1) & (leaving_slot == slot)
        columns.append(jnp.where(moving, moved_dest, jnp.where(live, stay_dest, junk[:, slot])))
    plan = jnp.stack(columns, 1).reshape(-1)
    return (counts.astype(jnp.int32), plan.astype(jnp.int32))


def draw_counts(key, part):
    return plan_draw(key)[0]


def draw_move_plan(key, part):
    return plan_draw(key)[1]


def shard_levels(own_key, extent, cuts, least, high):
    factor_of, own = 1.0, jax.random.fold_in(own_key, 6)
    for axis_at, blocks in cuts:
        draws = jnp.exp(jax.random.uniform(jax.random.fold_in(own, axis_at), (blocks,), jnp.float32, least / len(cuts), high / len(cuts)))
        factor_of = factor_of * jnp.repeat(draws, extent[axis_at] // blocks).reshape([-1 if axis == axis_at else 1 for axis in range(len(extent))])
    return factor_of


def normal_values(stream_key, shape, scale, reach, pieces=(), kind=jnp.bfloat16):
    loudness = shard_levels(stream_key, shape, pieces, -0.22, 0.18) if pieces else 1.0
    result = jax.random.normal(stream_key, shape, jnp.float32) * scale * loudness
    return jnp.minimum(jnp.maximum(result, -reach), reach).astype(kind)


def setup_inputs(seed: int = 0, part: int = 0) -> dict:
    arg_keys = jax.random.split(jax.random.key(seed), 18)
    own_keys = jax.random.split(jax.random.fold_in(arg_keys[17], part), 18)
    return {
        "counts": draw_counts(jax.random.fold_in(jax.random.fold_in(arg_keys[17], part), 71), part),
        "move_plan": draw_move_plan(jax.random.fold_in(jax.random.fold_in(arg_keys[17], part), 71), part),
        "ssm_state": normal_values(own_keys[2], (REQS, H, P_SIZE * N), 1.0, 6.0, ((0, 8), (1, 2)), jnp.float32),
        "conv_x_state": normal_values(own_keys[3], (REQS, 3, H * P_SIZE), 1.0, 6.0, ((0, 8), (2, 2))),
        "conv_bc_state": normal_values(own_keys[4], (REQS, 3, G, 2 * N), 1.0, 6.0, ((0, 8), (2, 2))),
        "x_in": normal_values(own_keys[5], (CAPS, STEPS, H * P_SIZE), 1.0, 6.0, ((0, 8), (2, 2))),
        "bc_in": normal_values(own_keys[6], (CAPS, STEPS, G, 2 * N), 1.0, 6.0, ((0, 8), (2, 2))),
        "z_in": normal_values(own_keys[7], (CAPS, STEPS, H * P_SIZE), 1.0, 6.0, ((0, 8), (2, 2))),
        "dt_in": normal_values(own_keys[8], (CAPS, STEPS, H), 0.5, 1.5, ((0, 8), (2, 2)), jnp.float32),
        "conv_w_x": normal_values(arg_keys[9], (4, H * P_SIZE), 4 ** -0.5, 3.0, ((1, 2),), jnp.float32),
        "conv_b_x": normal_values(arg_keys[10], (H * P_SIZE,), 0.5, 3.0, ((0, 2),), jnp.float32),
        "conv_w_bc": normal_values(arg_keys[11], (4, G, 2 * N), 4 ** -0.5, 3.0, ((1, 2),), jnp.float32),
        "conv_b_bc": normal_values(arg_keys[12], (G, 2 * N), 0.5, 3.0, ((0, 2),), jnp.float32),
        "dt_bias": jnp.clip(-4.0 + 3.0 * jax.random.uniform(arg_keys[13], (H,), jnp.float32) ** shard_levels(arg_keys[13], (H,), ((0, 2),), -0.2, 0.2), -4.0, -1.0),
        "a_log": jnp.clip(-2.5 + 2.0 * jax.random.uniform(arg_keys[14], (H,), jnp.float32) ** shard_levels(arg_keys[14], (H,), ((0, 2),), -0.2, 0.2), -2.5, -0.5),
        "d_skip": jnp.clip(0.3 + 1.2 * jax.random.uniform(arg_keys[15], (H,), jnp.float32) ** shard_levels(arg_keys[15], (H,), ((0, 2),), -0.2, 0.2), 0.3, 1.5),
        "norm_w": jnp.clip(1.0 + 0.18 * jax.random.normal(arg_keys[16], (H * P_SIZE,), jnp.float32), 0.1, 1.9),
    }


def plan_slots(counts, move_plan, caps):
    reqs = move_plan.shape[0]
    slots = reqs // counts.shape[0]
    ids = jnp.arange(reqs, dtype=jnp.int32)
    live = ids % slots < jnp.take(counts, ids // slots)
    targets = jnp.arange(caps, dtype=jnp.int32)
    match = live[None, :] & (move_plan[None, :] == targets[:, None])
    source = lax.optimization_barrier(jnp.sum(jnp.where(match, ids[None, :], 0), axis=1)).astype(jnp.int32)
    filled = jnp.any(match, axis=1)
    return (source, filled)

def reference(counts, move_plan, ssm_state, conv_x_state, conv_bc_state, x_in, bc_in, z_in, dt_in, conv_w_x, conv_b_x, conv_w_bc, conv_b_bc, dt_bias, a_log, d_skip, norm_w):
    caps = x_in.shape[0]
    source, filled = plan_slots(counts, move_plan, caps)
    per_group = H // G
    rate = jnp.exp(a_log)

    def one_slot(item):
        src, full, x_seq, bc_seq, z_seq, dt_seq = item
        state = jnp.take(ssm_state, src, axis=0).reshape(H, P_SIZE, N)
        state = jnp.where(full, state, jnp.zeros_like(state))
        conv_x = jnp.take(conv_x_state, src, axis=0)
        conv_x = jnp.where(full, conv_x, jnp.zeros_like(conv_x))
        conv_bc = jnp.take(conv_bc_state, src, axis=0)
        conv_bc = jnp.where(full, conv_bc, jnp.zeros_like(conv_bc))
        outputs = []
        for step in range(STEPS):
            x_new = x_seq[step]
            window = jnp.concatenate([conv_x, x_new[None]], 0).astype(jnp.float32)
            xconv = jax.nn.silu(lax.optimization_barrier(jnp.sum(window * conv_w_x, axis=0)) + conv_b_x)
            conv_x = jnp.concatenate([conv_x[1:], x_new[None]], 0)
            bc_new = bc_seq[step]
            bwindow = jnp.concatenate([conv_bc, bc_new[None]], 0).astype(jnp.float32)
            bconv = jax.nn.silu(lax.optimization_barrier(jnp.sum(bwindow * conv_w_bc, axis=0)) + conv_b_bc)
            conv_bc = jnp.concatenate([conv_bc[1:], bc_new[None]], 0)
            b_head = jnp.repeat(bconv[:, :N], per_group, axis=0)
            c_head = jnp.repeat(bconv[:, N:], per_group, axis=0)
            delta = jax.nn.softplus(dt_seq[step] + dt_bias)
            decay = jnp.exp(-delta * rate)
            heads_x = xconv.reshape(H, P_SIZE)
            state = decay[:, None, None] * state + (delta[:, None] * heads_x)[:, :, None] * b_head[:, None, :]
            mixed = lax.optimization_barrier(jnp.sum(state * c_head[:, None, :], axis=-1)) + d_skip[:, None] * heads_x
            gated = mixed.reshape(H * P_SIZE) * jax.nn.silu(z_seq[step].astype(jnp.float32))
            total = jnp.sum(gated * gated)
            normed = gated * lax.rsqrt(total / (H * P_SIZE) + 1e-05) * norm_w
            outputs.append(jnp.where(full, normed, jnp.zeros_like(normed)).astype(jnp.bfloat16))
        final = jnp.where(full, state.reshape(H, P_SIZE * N), jnp.zeros((H, P_SIZE * N), jnp.float32))
        conv_x = jnp.where(full, conv_x, jnp.zeros_like(conv_x))
        conv_bc = jnp.where(full, conv_bc, jnp.zeros_like(conv_bc))
        return (jnp.stack(outputs, 0), final, conv_x, conv_bc)
    y_out, new_ssm, new_conv_x, new_conv_bc = lax.map(one_slot, (source, filled, x_in, bc_in, z_in, dt_in))
    return (y_out, new_ssm, new_conv_x, new_conv_bc)
```

```python
import jax
import jax.numpy as jnp
from jax import lax
from jax.experimental import pallas as pl
from jax.experimental.pallas import tpu as pltpu
from jax.sharding import PartitionSpec as P

H = 128
P_SIZE = 64
STEPS = 4


def ssm_kernel(mask_ref, s_ref, u_ref, dec_ref, b_ref, c_ref, out_ref, y_ref):
    k = pl.program_id(0)
    rows, cols = s_ref.shape[1], s_ref.shape[2]
    seg = u_ref.shape[3]
    lane_seg = lax.broadcasted_iota(jnp.int32, (seg, cols), 1) // (cols // seg)
    expand = (lane_seg == lax.broadcasted_iota(jnp.int32, (seg, cols), 0)).astype(jnp.float32)
    state = s_ref[0]
    for t in range(STEPS):
        upd = jnp.dot(
            u_ref[0, t], expand, precision=lax.Precision.HIGHEST,
            preferred_element_type=jnp.float32,
        )
        state = dec_ref[0, t] * state + upd * b_ref[0, 0, t:t + 1, :]
        prod = state * c_ref[0, 0, t:t + 1, :]
        y_ref[0, t] = lax.dot_general(
            prod, expand, (((1,), (1,)), ((), ())), precision=lax.Precision.HIGHEST,
            preferred_element_type=jnp.float32,
        )
    out_ref[0] = state * mask_ref[k]


def ssm_steps(mask, state, u, dec, bt, ct):
    places, heads, cols = state.shape
    groups = bt.shape[1]
    per = heads // groups
    steps = u.shape[1]
    seg = u.shape[3]
    return pl.pallas_call(
        ssm_kernel,
        grid=(places, groups),
        in_specs=[
            pl.BlockSpec(memory_space=pltpu.SMEM),
            pl.BlockSpec((1, per, cols), lambda k, g: (k, g, 0)),
            pl.BlockSpec((1, steps, per, seg), lambda k, g: (k, 0, g, 0)),
            pl.BlockSpec((1, steps, per, 1), lambda k, g: (k, 0, g, 0)),
            pl.BlockSpec((1, 1, steps, cols), lambda k, g: (k, g, 0, 0)),
            pl.BlockSpec((1, 1, steps, cols), lambda k, g: (k, g, 0, 0)),
        ],
        out_specs=[
            pl.BlockSpec((1, per, cols), lambda k, g: (k, g, 0)),
            pl.BlockSpec((1, steps, per, seg), lambda k, g: (k, 0, g, 0)),
        ],
        out_shape=[
            jax.ShapeDtypeStruct(state.shape, jnp.float32),
            jax.ShapeDtypeStruct(u.shape, jnp.float32),
        ],
    )(mask, state, u, dec, bt, ct)


def migrate(counts, move_plan, ssm_state, conv_flat):
    owners = lax.axis_size("req")
    slots = ssm_state.shape[0]
    places = slots
    reqs = move_plan.shape[0]
    ids = jnp.arange(reqs, dtype=jnp.int32)
    home = ids // slots
    live = ids % slots < jnp.take(counts, home)
    zero_conv = jnp.zeros((), jnp.bfloat16)
    spread_state = lax.all_to_all(
        ssm_state.reshape(slots, owners, -1), "req", split_axis=1, concat_axis=0, tiled=True
    )
    spread_conv = lax.all_to_all(
        conv_flat.reshape(slots, owners, -1), "req", split_axis=1, concat_axis=0, tiled=True
    )
    targets = jnp.arange(owners * places, dtype=jnp.int32)
    match = live[None, :] & (move_plan[None, :] == targets[:, None])
    source = jnp.sum(jnp.where(match, ids[None, :], 0), axis=1)
    hit = jnp.any(match, axis=1)
    keep = hit.astype(jnp.float32)
    picked_state = jnp.take(spread_state, source, axis=0) * keep[:, None, None]
    picked_conv = jnp.where(hit[:, None, None], jnp.take(spread_conv, source, axis=0), zero_conv)
    arrived_state = lax.all_to_all(picked_state, "req", split_axis=0, concat_axis=1, tiled=True)
    arrived_conv = lax.all_to_all(picked_conv, "req", split_axis=0, concat_axis=1, tiled=True)
    owner = lax.axis_index("req")
    mask = lax.dynamic_slice_in_dim(keep, owner * places, places)
    return arrived_state.reshape(ssm_state.shape), arrived_conv.reshape(conv_flat.shape), mask


def on_device(
    counts,
    move_plan,
    ssm_state,
    conv_x_state,
    conv_bc_state,
    x_in,
    bc_in,
    z_in,
    dt_in,
    conv_w_x,
    conv_b_x,
    conv_w_bc,
    conv_b_bc,
    dt_bias,
    a_log,
    d_skip,
    norm_w,
):
    slots, heads_loc, columns = ssm_state.shape
    places, steps, channels = x_in.shape
    groups_loc = conv_bc_state.shape[2]
    pair = conv_bc_state.shape[3]
    state_size = pair // 2
    head_dim = channels // heads_loc
    conv_flat = jnp.concatenate(
        [conv_x_state.reshape(slots, -1), conv_bc_state.reshape(slots, -1)], 1
    )
    state, conv, mask = migrate(counts, move_plan, ssm_state, conv_flat)
    conv_x = conv[:, : 3 * channels].reshape(places, 3, channels)
    conv_bc = conv[:, 3 * channels :].reshape(places, 3, groups_loc, pair)
    per_group = heads_loc // groups_loc

    seq_x = jnp.concatenate([conv_x, x_in], 1)
    seq_bc = jnp.concatenate([conv_bc, bc_in], 1)
    wx = seq_x.astype(jnp.float32)
    wbc = seq_bc.astype(jnp.float32)
    xconv = conv_b_x + sum(wx[:, k:k + steps] * conv_w_x[k] for k in range(4))
    xconv = jax.nn.silu(xconv)
    bconv = conv_b_bc + sum(wbc[:, k:k + steps] * conv_w_bc[k] for k in range(4))
    bconv = jax.nn.silu(bconv)
    delta = jax.nn.softplus(dt_in + dt_bias)
    decay = jnp.exp(-delta * jnp.exp(a_log))
    heads_x = xconv.reshape(places, steps, heads_loc, head_dim)
    u = delta[..., None] * heads_x
    dec = decay[..., None]
    reps = columns // state_size
    bt = jnp.tile(bconv[..., :state_size], (1, 1, 1, reps)).transpose(0, 2, 1, 3)
    ct = jnp.tile(bconv[..., state_size:], (1, 1, 1, reps)).transpose(0, 2, 1, 3)
    new_state, yk = ssm_steps(mask, state, u, dec, bt, ct)
    mixed = yk + d_skip[None, None, :, None] * heads_x
    gated = mixed.reshape(places, steps, channels) * jax.nn.silu(z_in.astype(jnp.float32))
    total = lax.psum(jnp.sum(gated * gated, axis=-1), "tp")
    scaling = 1.0 / (H * P_SIZE)
    normed = gated * lax.rsqrt(total * scaling + 1e-05)[..., None] * norm_w
    y_out = (normed * mask[:, None, None]).astype(jnp.bfloat16)
    filled = mask > 0.5
    new_conv_x = jnp.where(filled[:, None, None], seq_x[:, steps:], jnp.zeros((), jnp.bfloat16))
    new_conv_bc = jnp.where(
        filled[:, None, None, None], seq_bc[:, steps:], jnp.zeros((), jnp.bfloat16)
    )
    return (y_out, new_state, new_conv_x, new_conv_bc)


def solution(mesh):
    in_specs = (
        P("parts"),
        P("parts"),
        P(("parts", "req"), "tp", None),
        P(("parts", "req"), None, "tp"),
        P(("parts", "req"), None, "tp", None),
        P(("parts", "req"), None, "tp"),
        P(("parts", "req"), None, "tp", None),
        P(("parts", "req"), None, "tp"),
        P(("parts", "req"), None, "tp"),
        P(None, "tp"),
        P("tp"),
        P(None, "tp", None),
        P("tp", None),
        P("tp"),
        P("tp"),
        P("tp"),
        P("tp"),
    )
    out_specs = (
        P(("parts", "req"), None, "tp"),
        P(("parts", "req"), "tp", None),
        P(("parts", "req"), None, "tp"),
        P(("parts", "req"), None, "tp", None),
    )
    return jax.shard_map(
        on_device, mesh=mesh, in_specs=in_specs, out_specs=out_specs, check_vma=False
    )
```

```python
import jax
import jax.numpy as jnp
from jax import lax
from jax.experimental import pallas as pl
from jax.experimental.pallas import tpu as pltpu
from jax.sharding import PartitionSpec as P

H = 128
P_SIZE = 64
STEPS = 4


def ssm_kernel(sel_ref, s_ref, r_ref, u_ref, dec_ref, b_ref, c_ref, out_ref, y_ref):
    k = pl.program_id(0)
    places = pl.num_programs(0)
    rows, cols = s_ref.shape[1], s_ref.shape[2]
    seg = u_ref.shape[3]
    lane_seg = lax.broadcasted_iota(jnp.int32, (seg, cols), 1) // (cols // seg)
    expand = (lane_seg == lax.broadcasted_iota(jnp.int32, (seg, cols), 0)).astype(jnp.float32)
    state = jnp.where(sel_ref[places + k] == 1, r_ref[0], s_ref[0])
    for t in range(STEPS):
        upd = jnp.dot(
            u_ref[0, t], expand, precision=lax.Precision.HIGHEST,
            preferred_element_type=jnp.float32,
        )
        state = dec_ref[0, t] * state + upd * b_ref[0, 0, t:t + 1, :]
        prod = state * c_ref[0, 0, t:t + 1, :]
        y_ref[0, t] = lax.dot_general(
            prod, expand, (((1,), (1,)), ((), ())), precision=lax.Precision.HIGHEST,
            preferred_element_type=jnp.float32,
        )
    keep = (sel_ref[2 * places + k] == 1).astype(jnp.float32)
    out_ref[0] = state * keep


def ssm_steps(sel, state, recv, u, dec, bt, ct):
    places, heads, cols = state.shape
    groups = bt.shape[1]
    per = heads // groups
    steps = u.shape[1]
    seg = u.shape[3]
    grid_spec = pltpu.PrefetchScalarGridSpec(
        num_scalar_prefetch=1,
        grid=(places, groups),
        in_specs=[
            pl.BlockSpec((1, per, cols), lambda k, g, s: (s[k], g, 0)),
            pl.BlockSpec((1, per, cols), lambda k, g, s: (0, g, 0)),
            pl.BlockSpec((1, steps, per, seg), lambda k, g, s: (k, 0, g, 0)),
            pl.BlockSpec((1, steps, per, 1), lambda k, g, s: (k, 0, g, 0)),
            pl.BlockSpec((1, 1, steps, cols), lambda k, g, s: (k, g, 0, 0)),
            pl.BlockSpec((1, 1, steps, cols), lambda k, g, s: (k, g, 0, 0)),
        ],
        out_specs=[
            pl.BlockSpec((1, per, cols), lambda k, g, s: (k, g, 0)),
            pl.BlockSpec((1, steps, per, seg), lambda k, g, s: (k, 0, g, 0)),
        ],
    )
    return pl.pallas_call(
        ssm_kernel,
        grid_spec=grid_spec,
        out_shape=[
            jax.ShapeDtypeStruct(state.shape, jnp.float32),
            jax.ShapeDtypeStruct(u.shape, jnp.float32),
        ],
    )(sel, state, recv, u, dec, bt, ct)


def migrate(counts, move_plan, ssm_state, conv_flat):
    owners = lax.axis_size("req")
    slots = ssm_state.shape[0]
    reqs = move_plan.shape[0]
    owner = lax.axis_index("req")
    ids = jnp.arange(reqs, dtype=jnp.int32)
    home = ids // slots
    live = ids % slots < jnp.take(counts, home)
    dest_owner = move_plan // slots
    outgoing = live & (home == owner) & (dest_owner != owner)
    send_j = jnp.sum(jnp.where(outgoing, ids, 0)) % slots
    owner_ids = jnp.arange(owners, dtype=jnp.int32)
    incoming = (
        live[None, :]
        & (dest_owner[None, :] == owner_ids[:, None])
        & (home[None, :] != owner_ids[:, None])
    )
    src_owner = jnp.sum(jnp.where(incoming, ids[None, :], 0), axis=1) // slots
    out_state = lax.dynamic_index_in_dim(ssm_state, send_j, 0, keepdims=False)
    out_conv = lax.dynamic_index_in_dim(conv_flat, send_j, 0, keepdims=False)
    spread_state = lax.all_to_all(
        out_state.reshape(owners, -1), "req", split_axis=0, concat_axis=0, tiled=True
    )
    spread_conv = lax.all_to_all(
        out_conv.reshape(owners, -1), "req", split_axis=0, concat_axis=0, tiled=True
    )
    picked_state = jnp.take(spread_state, src_owner, axis=0)
    picked_conv = jnp.take(spread_conv, src_owner, axis=0)
    rstate = lax.all_to_all(picked_state, "req", split_axis=0, concat_axis=0, tiled=True)
    rconv = lax.all_to_all(picked_conv, "req", split_axis=0, concat_axis=0, tiled=True)
    rstate = rstate.reshape((1,) + ssm_state.shape[1:])
    rconv = rconv.reshape(1, -1)
    targets = owner * slots + jnp.arange(slots, dtype=jnp.int32)
    match = live[None, :] & (move_plan[None, :] == targets[:, None])
    hit = jnp.any(match, axis=1)
    source = jnp.sum(jnp.where(match, ids[None, :], 0), axis=1)
    use_recv = hit & (source // slots != owner)
    local = jnp.where(hit & ~use_recv, source % slots, 0)
    sel = jnp.concatenate([local, use_recv.astype(jnp.int32), hit.astype(jnp.int32)])
    conv = jnp.where(use_recv[:, None], rconv, jnp.take(conv_flat, local, axis=0))
    return sel, rstate, conv, hit.astype(jnp.float32)


def on_device(
    counts,
    move_plan,
    ssm_state,
    conv_x_state,
    conv_bc_state,
    x_in,
    bc_in,
    z_in,
    dt_in,
    conv_w_x,
    conv_b_x,
    conv_w_bc,
    conv_b_bc,
    dt_bias,
    a_log,
    d_skip,
    norm_w,
):
    slots, heads_loc, columns = ssm_state.shape
    places, steps, channels = x_in.shape
    groups_loc = conv_bc_state.shape[2]
    pair = conv_bc_state.shape[3]
    state_size = pair // 2
    head_dim = channels // heads_loc
    conv_flat = jnp.concatenate(
        [conv_x_state.reshape(slots, -1), conv_bc_state.reshape(slots, -1)], 1
    )
    sel, recv, conv, mask = migrate(counts, move_plan, ssm_state, conv_flat)
    conv_x = conv[:, : 3 * channels].reshape(places, 3, channels)
    conv_bc = conv[:, 3 * channels :].reshape(places, 3, groups_loc, pair)
    per_group = heads_loc // groups_loc

    seq_x = jnp.concatenate([conv_x, x_in], 1)
    seq_bc = jnp.concatenate([conv_bc, bc_in], 1)
    wx = seq_x.astype(jnp.float32)
    wbc = seq_bc.astype(jnp.float32)
    xconv = conv_b_x + sum(wx[:, k:k + steps] * conv_w_x[k] for k in range(4))
    xconv = jax.nn.silu(xconv)
    bconv = conv_b_bc + sum(wbc[:, k:k + steps] * conv_w_bc[k] for k in range(4))
    bconv = jax.nn.silu(bconv)
    delta = jax.nn.softplus(dt_in + dt_bias)
    decay = jnp.exp(-delta * jnp.exp(a_log))
    heads_x = xconv.reshape(places, steps, heads_loc, head_dim)
    u = delta[..., None] * heads_x
    dec = decay[..., None]
    reps = columns // state_size
    bt = jnp.tile(bconv[..., :state_size], (1, 1, 1, reps)).transpose(0, 2, 1, 3)
    ct = jnp.tile(bconv[..., state_size:], (1, 1, 1, reps)).transpose(0, 2, 1, 3)
    new_state, yk = ssm_steps(sel, ssm_state, recv, u, dec, bt, ct)
    mixed = yk + d_skip[None, None, :, None] * heads_x
    gated = mixed.reshape(places, steps, channels) * jax.nn.silu(z_in.astype(jnp.float32))
    total = lax.psum(jnp.sum(gated * gated, axis=-1), "tp")
    scaling = 1.0 / (H * P_SIZE)
    normed = gated * lax.rsqrt(total * scaling + 1e-05)[..., None] * norm_w
    y_out = (normed * mask[:, None, None]).astype(jnp.bfloat16)
    filled = mask > 0.5
    new_conv_x = jnp.where(filled[:, None, None], seq_x[:, steps:], jnp.zeros((), jnp.bfloat16))
    new_conv_bc = jnp.where(
        filled[:, None, None, None], seq_bc[:, steps:], jnp.zeros((), jnp.bfloat16)
    )
    return (y_out, new_state, new_conv_x, new_conv_bc)


def solution(mesh):
    in_specs = (
        P("parts"),
        P("parts"),
        P(("parts", "req"), "tp", None),
        P(("parts", "req"), None, "tp"),
        P(("parts", "req"), None, "tp", None),
        P(("parts", "req"), None, "tp"),
        P(("parts", "req"), None, "tp", None),
        P(("parts", "req"), None, "tp"),
        P(("parts", "req"), None, "tp"),
        P(None, "tp"),
        P("tp"),
        P(None, "tp", None),
        P("tp", None),
        P("tp"),
        P("tp"),
        P("tp"),
        P("tp"),
    )
    out_specs = (
        P(("parts", "req"), None, "tp"),
        P(("parts", "req"), "tp", None),
        P(("parts", "req"), None, "tp"),
        P(("parts", "req"), None, "tp", None),
    )
    return jax.shard_map(
        on_device, mesh=mesh, in_specs=in_specs, out_specs=out_specs, check_vma=False
    )
```

```python
import jax
import jax.numpy as jnp
from jax import lax
from jax.experimental import pallas as pl
from jax.experimental.pallas import tpu as pltpu
from jax.sharding import PartitionSpec as P

H = 128
P_SIZE = 64
STEPS = 4


def ssm_kernel(sel_ref, s_ref, r_ref, u_ref, dec_ref, b_ref, c_ref, out_ref, y_ref):
    k = pl.program_id(0)
    places = pl.num_programs(0)
    rows, cols = s_ref.shape[1], s_ref.shape[2]
    seg = u_ref.shape[3]
    lane_seg = lax.broadcasted_iota(jnp.int32, (seg, cols), 1) // (cols // seg)
    expand = (lane_seg == lax.broadcasted_iota(jnp.int32, (seg, cols), 0)).astype(jnp.float32)
    state = jnp.where(sel_ref[places + k] == 1, r_ref[0], s_ref[0])
    for t in range(STEPS):
        upd = jnp.dot(
            u_ref[0, t], expand, precision=lax.Precision.HIGHEST,
            preferred_element_type=jnp.float32,
        )
        state = dec_ref[0, t] * state + upd * b_ref[0, 0, t:t + 1, :]
        prod = state * c_ref[0, 0, t:t + 1, :]
        y_ref[0, t] = lax.dot_general(
            prod, expand, (((1,), (1,)), ((), ())), precision=lax.Precision.HIGHEST,
            preferred_element_type=jnp.float32,
        )
    keep = (sel_ref[2 * places + k] == 1).astype(jnp.float32)
    out_ref[0] = state * keep


def ssm_steps(sel, state, recv, u, dec, bt, ct):
    places, heads, cols = state.shape
    groups = bt.shape[1]
    per = heads // groups
    steps = u.shape[1]
    seg = u.shape[3]
    grid_spec = pltpu.PrefetchScalarGridSpec(
        num_scalar_prefetch=1,
        grid=(places, groups),
        in_specs=[
            pl.BlockSpec((1, per, cols), lambda k, g, s: (s[k], g, 0)),
            pl.BlockSpec((1, per, cols), lambda k, g, s: (0, g, 0)),
            pl.BlockSpec((1, steps, per, seg), lambda k, g, s: (k, 0, g, 0)),
            pl.BlockSpec((1, steps, per, 1), lambda k, g, s: (k, 0, g, 0)),
            pl.BlockSpec((1, 1, steps, cols), lambda k, g, s: (k, g, 0, 0)),
            pl.BlockSpec((1, 1, steps, cols), lambda k, g, s: (k, g, 0, 0)),
        ],
        out_specs=[
            pl.BlockSpec((1, per, cols), lambda k, g, s: (k, g, 0)),
            pl.BlockSpec((1, steps, per, seg), lambda k, g, s: (k, 0, g, 0)),
        ],
    )
    return pl.pallas_call(
        ssm_kernel,
        grid_spec=grid_spec,
        out_shape=[
            jax.ShapeDtypeStruct(state.shape, jnp.float32),
            jax.ShapeDtypeStruct(u.shape, jnp.float32),
        ],
    )(sel, state, recv, u, dec, bt, ct)


def migrate(counts, move_plan, ssm_state, conv_flat):
    owners = lax.axis_size("req")
    slots = ssm_state.shape[0]
    reqs = move_plan.shape[0]
    owner = lax.axis_index("req")
    ids = jnp.arange(reqs, dtype=jnp.int32)
    home = ids // slots
    live = ids % slots < jnp.take(counts, home)
    dest_owner = move_plan // slots
    outgoing = live & (home == owner) & (dest_owner != owner)
    send_j = jnp.sum(jnp.where(outgoing, ids, 0)) % slots
    owner_ids = jnp.arange(owners, dtype=jnp.int32)
    incoming = (
        live[None, :]
        & (dest_owner[None, :] == owner_ids[:, None])
        & (home[None, :] != owner_ids[:, None])
    )
    src_owner = jnp.sum(jnp.where(incoming, ids[None, :], 0), axis=1) // slots
    out_state = lax.dynamic_index_in_dim(ssm_state, send_j, 0, keepdims=False)
    out_conv = lax.dynamic_index_in_dim(conv_flat, send_j, 0, keepdims=False)
    state_words = out_state.reshape(owners, -1)
    conv_words = out_conv.astype(jnp.float32).reshape(owners, -1)
    split = state_words.shape[1]
    packed = jnp.concatenate([state_words, conv_words], 1)
    spread = lax.all_to_all(packed, "req", split_axis=0, concat_axis=0, tiled=True)
    picked = jnp.take(spread, src_owner, axis=0)
    arrived = lax.all_to_all(picked, "req", split_axis=0, concat_axis=0, tiled=True)
    rstate = arrived[:, :split].reshape((1,) + ssm_state.shape[1:])
    rconv = arrived[:, split:].astype(jnp.bfloat16).reshape(1, -1)
    targets = owner * slots + jnp.arange(slots, dtype=jnp.int32)
    match = live[None, :] & (move_plan[None, :] == targets[:, None])
    hit = jnp.any(match, axis=1)
    source = jnp.sum(jnp.where(match, ids[None, :], 0), axis=1)
    use_recv = hit & (source // slots != owner)
    local = jnp.where(hit & ~use_recv, source % slots, 0)
    sel = jnp.concatenate([local, use_recv.astype(jnp.int32), hit.astype(jnp.int32)])
    conv = jnp.where(use_recv[:, None], rconv, jnp.take(conv_flat, local, axis=0))
    return sel, rstate, conv, hit.astype(jnp.float32)


def on_device(
    counts,
    move_plan,
    ssm_state,
    conv_x_state,
    conv_bc_state,
    x_in,
    bc_in,
    z_in,
    dt_in,
    conv_w_x,
    conv_b_x,
    conv_w_bc,
    conv_b_bc,
    dt_bias,
    a_log,
    d_skip,
    norm_w,
):
    slots, heads_loc, columns = ssm_state.shape
    places, steps, channels = x_in.shape
    groups_loc = conv_bc_state.shape[2]
    pair = conv_bc_state.shape[3]
    state_size = pair // 2
    head_dim = channels // heads_loc
    conv_flat = jnp.concatenate(
        [conv_x_state.reshape(slots, -1), conv_bc_state.reshape(slots, -1)], 1
    )
    sel, recv, conv, mask = migrate(counts, move_plan, ssm_state, conv_flat)
    conv_x = conv[:, : 3 * channels].reshape(places, 3, channels)
    conv_bc = conv[:, 3 * channels :].reshape(places, 3, groups_loc, pair)
    per_group = heads_loc // groups_loc

    seq_x = jnp.concatenate([conv_x, x_in], 1)
    seq_bc = jnp.concatenate([conv_bc, bc_in], 1)
    wx = seq_x.astype(jnp.float32)
    wbc = seq_bc.astype(jnp.float32)
    xconv = conv_b_x + sum(wx[:, k:k + steps] * conv_w_x[k] for k in range(4))
    xconv = jax.nn.silu(xconv)
    bconv = conv_b_bc + sum(wbc[:, k:k + steps] * conv_w_bc[k] for k in range(4))
    bconv = jax.nn.silu(bconv)
    delta = jax.nn.softplus(dt_in + dt_bias)
    decay = jnp.exp(-delta * jnp.exp(a_log))
    heads_x = xconv.reshape(places, steps, heads_loc, head_dim)
    u = delta[..., None] * heads_x
    dec = decay[..., None]
    reps = columns // state_size
    bt = jnp.tile(bconv[..., :state_size], (1, 1, 1, reps)).transpose(0, 2, 1, 3)
    ct = jnp.tile(bconv[..., state_size:], (1, 1, 1, reps)).transpose(0, 2, 1, 3)
    new_state, yk = ssm_steps(sel, ssm_state, recv, u, dec, bt, ct)
    mixed = yk + d_skip[None, None, :, None] * heads_x
    gated = mixed.reshape(places, steps, channels) * jax.nn.silu(z_in.astype(jnp.float32))
    total = lax.psum(jnp.sum(gated * gated, axis=-1), "tp")
    scaling = 1.0 / (H * P_SIZE)
    normed = gated * lax.rsqrt(total * scaling + 1e-05)[..., None] * norm_w
    y_out = (normed * mask[:, None, None]).astype(jnp.bfloat16)
    filled = mask > 0.5
    new_conv_x = jnp.where(filled[:, None, None], seq_x[:, steps:], jnp.zeros((), jnp.bfloat16))
    new_conv_bc = jnp.where(
        filled[:, None, None, None], seq_bc[:, steps:], jnp.zeros((), jnp.bfloat16)
    )
    return (y_out, new_state, new_conv_x, new_conv_bc)


def solution(mesh):
    in_specs = (
        P("parts"),
        P("parts"),
        P(("parts", "req"), "tp", None),
        P(("parts", "req"), None, "tp"),
        P(("parts", "req"), None, "tp", None),
        P(("parts", "req"), None, "tp"),
        P(("parts", "req"), None, "tp", None),
        P(("parts", "req"), None, "tp"),
        P(("parts", "req"), None, "tp"),
        P(None, "tp"),
        P("tp"),
        P(None, "tp", None),
        P("tp", None),
        P("tp"),
        P("tp"),
        P("tp"),
        P("tp"),
    )
    out_specs = (
        P(("parts", "req"), None, "tp"),
        P(("parts", "req"), "tp", None),
        P(("parts", "req"), None, "tp"),
        P(("parts", "req"), None, "tp", None),
    )
    return jax.shard_map(
        on_device, mesh=mesh, in_specs=in_specs, out_specs=out_specs, check_vma=False
    )
```

```python
import jax
import jax.numpy as jnp
from jax import lax
from jax.experimental import pallas as pl
from jax.experimental.pallas import tpu as pltpu
from jax.sharding import PartitionSpec as P

H = 128
P_SIZE = 64
STEPS = 4


def ssm_kernel(sel_ref, s_ref, r_ref, u_ref, dec_ref, b_ref, c_ref, out_ref, y_ref):
    k = pl.program_id(0)
    places = pl.num_programs(0)
    rows, cols = s_ref.shape[1], s_ref.shape[2]
    seg = u_ref.shape[3]
    lane_seg = lax.broadcasted_iota(jnp.int32, (seg, cols), 1) // (cols // seg)
    expand = (lane_seg == lax.broadcasted_iota(jnp.int32, (seg, cols), 0)).astype(jnp.bfloat16)
    state = jnp.where(sel_ref[places + k] == 1, r_ref[0], s_ref[0])
    for t in range(STEPS):
        u = u_ref[0, t]
        u_hi = u.astype(jnp.bfloat16)
        u_lo = (u - u_hi.astype(jnp.float32)).astype(jnp.bfloat16)
        upd = jnp.dot(u_hi, expand, preferred_element_type=jnp.float32) + jnp.dot(
            u_lo, expand, preferred_element_type=jnp.float32
        )
        state = dec_ref[0, t] * state + upd * b_ref[0, 0, t:t + 1, :]
        prod = state * c_ref[0, 0, t:t + 1, :]
        p_hi = prod.astype(jnp.bfloat16)
        p_lo = (prod - p_hi.astype(jnp.float32)).astype(jnp.bfloat16)
        dims = (((1,), (1,)), ((), ()))
        y_ref[0, t] = lax.dot_general(
            p_hi, expand, dims, preferred_element_type=jnp.float32
        ) + lax.dot_general(p_lo, expand, dims, preferred_element_type=jnp.float32)
    keep = (sel_ref[2 * places + k] == 1).astype(jnp.float32)
    out_ref[0] = state * keep


def ssm_steps(sel, state, recv, u, dec, bt, ct):
    places, heads, cols = state.shape
    groups = bt.shape[1]
    per = heads // groups
    steps = u.shape[1]
    seg = u.shape[3]
    grid_spec = pltpu.PrefetchScalarGridSpec(
        num_scalar_prefetch=1,
        grid=(places, groups),
        in_specs=[
            pl.BlockSpec((1, per, cols), lambda k, g, s: (s[k], g, 0)),
            pl.BlockSpec((1, per, cols), lambda k, g, s: (0, g, 0)),
            pl.BlockSpec((1, steps, per, seg), lambda k, g, s: (k, 0, g, 0)),
            pl.BlockSpec((1, steps, per, 1), lambda k, g, s: (k, 0, g, 0)),
            pl.BlockSpec((1, 1, steps, cols), lambda k, g, s: (k, g, 0, 0)),
            pl.BlockSpec((1, 1, steps, cols), lambda k, g, s: (k, g, 0, 0)),
        ],
        out_specs=[
            pl.BlockSpec((1, per, cols), lambda k, g, s: (k, g, 0)),
            pl.BlockSpec((1, steps, per, seg), lambda k, g, s: (k, 0, g, 0)),
        ],
    )
    return pl.pallas_call(
        ssm_kernel,
        grid_spec=grid_spec,
        out_shape=[
            jax.ShapeDtypeStruct(state.shape, jnp.float32),
            jax.ShapeDtypeStruct(u.shape, jnp.float32),
        ],
    )(sel, state, recv, u, dec, bt, ct)


def migrate(counts, move_plan, ssm_state, conv_flat):
    owners = lax.axis_size("req")
    slots = ssm_state.shape[0]
    reqs = move_plan.shape[0]
    owner = lax.axis_index("req")
    ids = jnp.arange(reqs, dtype=jnp.int32)
    home = ids // slots
    live = ids % slots < jnp.take(counts, home)
    dest_owner = move_plan // slots
    outgoing = live & (home == owner) & (dest_owner != owner)
    send_j = jnp.sum(jnp.where(outgoing, ids, 0)) % slots
    owner_ids = jnp.arange(owners, dtype=jnp.int32)
    incoming = (
        live[None, :]
        & (dest_owner[None, :] == owner_ids[:, None])
        & (home[None, :] != owner_ids[:, None])
    )
    src_owner = jnp.sum(jnp.where(incoming, ids[None, :], 0), axis=1) // slots
    out_state = lax.dynamic_index_in_dim(ssm_state, send_j, 0, keepdims=False)
    out_conv = lax.dynamic_index_in_dim(conv_flat, send_j, 0, keepdims=False)
    state_words = out_state.reshape(owners, -1)
    conv_words = out_conv.astype(jnp.float32).reshape(owners, -1)
    split = state_words.shape[1]
    packed = jnp.concatenate([state_words, conv_words], 1)
    spread = lax.all_to_all(packed, "req", split_axis=0, concat_axis=0, tiled=True)
    picked = jnp.take(spread, src_owner, axis=0)
    arrived = lax.all_to_all(picked, "req", split_axis=0, concat_axis=0, tiled=True)
    rstate = arrived[:, :split].reshape((1,) + ssm_state.shape[1:])
    rconv = arrived[:, split:].astype(jnp.bfloat16).reshape(1, -1)
    targets = owner * slots + jnp.arange(slots, dtype=jnp.int32)
    match = live[None, :] & (move_plan[None, :] == targets[:, None])
    hit = jnp.any(match, axis=1)
    source = jnp.sum(jnp.where(match, ids[None, :], 0), axis=1)
    use_recv = hit & (source // slots != owner)
    local = jnp.where(hit & ~use_recv, source % slots, 0)
    sel = jnp.concatenate([local, use_recv.astype(jnp.int32), hit.astype(jnp.int32)])
    conv = jnp.where(use_recv[:, None], rconv, jnp.take(conv_flat, local, axis=0))
    return sel, rstate, conv, hit.astype(jnp.float32)


def on_device(
    counts,
    move_plan,
    ssm_state,
    conv_x_state,
    conv_bc_state,
    x_in,
    bc_in,
    z_in,
    dt_in,
    conv_w_x,
    conv_b_x,
    conv_w_bc,
    conv_b_bc,
    dt_bias,
    a_log,
    d_skip,
    norm_w,
):
    slots, heads_loc, columns = ssm_state.shape
    places, steps, channels = x_in.shape
    groups_loc = conv_bc_state.shape[2]
    pair = conv_bc_state.shape[3]
    state_size = pair // 2
    head_dim = channels // heads_loc
    conv_flat = jnp.concatenate(
        [conv_x_state.reshape(slots, -1), conv_bc_state.reshape(slots, -1)], 1
    )
    sel, recv, conv, mask = migrate(counts, move_plan, ssm_state, conv_flat)
    conv_x = conv[:, : 3 * channels].reshape(places, 3, channels)
    conv_bc = conv[:, 3 * channels :].reshape(places, 3, groups_loc, pair)
    per_group = heads_loc // groups_loc

    seq_x = jnp.concatenate([conv_x, x_in], 1)
    seq_bc = jnp.concatenate([conv_bc, bc_in], 1)
    wx = seq_x.astype(jnp.float32)
    wbc = seq_bc.astype(jnp.float32)
    xconv = conv_b_x + sum(wx[:, k:k + steps] * conv_w_x[k] for k in range(4))
    xconv = jax.nn.silu(xconv)
    bconv = conv_b_bc + sum(wbc[:, k:k + steps] * conv_w_bc[k] for k in range(4))
    bconv = jax.nn.silu(bconv)
    delta = jax.nn.softplus(dt_in + dt_bias)
    decay = jnp.exp(-delta * jnp.exp(a_log))
    heads_x = xconv.reshape(places, steps, heads_loc, head_dim)
    u = delta[..., None] * heads_x
    dec = decay[..., None]
    reps = columns // state_size
    bt = jnp.tile(bconv[..., :state_size], (1, 1, 1, reps)).transpose(0, 2, 1, 3)
    ct = jnp.tile(bconv[..., state_size:], (1, 1, 1, reps)).transpose(0, 2, 1, 3)
    new_state, yk = ssm_steps(sel, ssm_state, recv, u, dec, bt, ct)
    mixed = yk + d_skip[None, None, :, None] * heads_x
    gated = mixed.reshape(places, steps, channels) * jax.nn.silu(z_in.astype(jnp.float32))
    total = lax.psum(jnp.sum(gated * gated, axis=-1), "tp")
    scaling = 1.0 / (H * P_SIZE)
    normed = gated * lax.rsqrt(total * scaling + 1e-05)[..., None] * norm_w
    y_out = (normed * mask[:, None, None]).astype(jnp.bfloat16)
    filled = mask > 0.5
    new_conv_x = jnp.where(filled[:, None, None], seq_x[:, steps:], jnp.zeros((), jnp.bfloat16))
    new_conv_bc = jnp.where(
        filled[:, None, None, None], seq_bc[:, steps:], jnp.zeros((), jnp.bfloat16)
    )
    return (y_out, new_state, new_conv_x, new_conv_bc)


def solution(mesh):
    in_specs = (
        P("parts"),
        P("parts"),
        P(("parts", "req"), "tp", None),
        P(("parts", "req"), None, "tp"),
        P(("parts", "req"), None, "tp", None),
        P(("parts", "req"), None, "tp"),
        P(("parts", "req"), None, "tp", None),
        P(("parts", "req"), None, "tp"),
        P(("parts", "req"), None, "tp"),
        P(None, "tp"),
        P("tp"),
        P(None, "tp", None),
        P("tp", None),
        P("tp"),
        P("tp"),
        P("tp"),
        P("tp"),
    )
    out_specs = (
        P(("parts", "req"), None, "tp"),
        P(("parts", "req"), "tp", None),
        P(("parts", "req"), None, "tp"),
        P(("parts", "req"), None, "tp", None),
    )
    return jax.shard_map(
        on_device, mesh=mesh, in_specs=in_specs, out_specs=out_specs, check_vma=False
    )
```

```python
import jax
import jax.numpy as jnp
from jax import lax
from jax.experimental import pallas as pl
from jax.experimental.pallas import tpu as pltpu
from jax.sharding import PartitionSpec as P

H = 128
P_SIZE = 64
STEPS = 4


def ssm_kernel(sel_ref, s_ref, r_ref, u_ref, dec_ref, b_ref, c_ref, out_ref, y_ref):
    k = pl.program_id(0)
    places = pl.num_programs(0)
    rows, cols = s_ref.shape[1], s_ref.shape[2]
    seg = u_ref.shape[3]
    lane_seg = lax.broadcasted_iota(jnp.int32, (seg, cols), 1) // (cols // seg)
    expand = (lane_seg == lax.broadcasted_iota(jnp.int32, (seg, cols), 0)).astype(jnp.bfloat16)
    state = jnp.where(sel_ref[places + k] == 1, r_ref[0], s_ref[0])
    for t in range(STEPS):
        u = u_ref[0, t]
        u_hi = u.astype(jnp.bfloat16)
        u_lo = (u - u_hi.astype(jnp.float32)).astype(jnp.bfloat16)
        upd = jnp.dot(u_hi, expand, preferred_element_type=jnp.float32) + jnp.dot(
            u_lo, expand, preferred_element_type=jnp.float32
        )
        state = dec_ref[0, t] * state + upd * b_ref[0, 0, t:t + 1, :]
        prod = state * c_ref[0, 0, t:t + 1, :]
        p_hi = prod.astype(jnp.bfloat16)
        p_lo = (prod - p_hi.astype(jnp.float32)).astype(jnp.bfloat16)
        dims = (((1,), (1,)), ((), ()))
        y_ref[0, t] = lax.dot_general(
            p_hi, expand, dims, preferred_element_type=jnp.float32
        ) + lax.dot_general(p_lo, expand, dims, preferred_element_type=jnp.float32)
    keep = (sel_ref[2 * places + k] == 1).astype(jnp.float32)
    out_ref[0] = state * keep


def ssm_steps(sel, state, recv, u, dec, bt, ct):
    places, heads, cols = state.shape
    groups = bt.shape[1]
    per = heads // groups
    steps = u.shape[1]
    seg = u.shape[3]
    grid_spec = pltpu.PrefetchScalarGridSpec(
        num_scalar_prefetch=1,
        grid=(places, groups),
        in_specs=[
            pl.BlockSpec((1, per, cols), lambda k, g, s: (s[k], g, 0)),
            pl.BlockSpec((1, per, cols), lambda k, g, s: (0, g, 0)),
            pl.BlockSpec((1, steps, per, seg), lambda k, g, s: (k, 0, g, 0)),
            pl.BlockSpec((1, steps, per, 1), lambda k, g, s: (k, 0, g, 0)),
            pl.BlockSpec((1, 1, steps, cols), lambda k, g, s: (k, g, 0, 0)),
            pl.BlockSpec((1, 1, steps, cols), lambda k, g, s: (k, g, 0, 0)),
        ],
        out_specs=[
            pl.BlockSpec((1, per, cols), lambda k, g, s: (k, g, 0)),
            pl.BlockSpec((1, steps, per, seg), lambda k, g, s: (k, 0, g, 0)),
        ],
    )
    return pl.pallas_call(
        ssm_kernel,
        grid_spec=grid_spec,
        out_shape=[
            jax.ShapeDtypeStruct(state.shape, jnp.float32),
            jax.ShapeDtypeStruct(u.shape, jnp.float32),
        ],
    )(sel, state, recv, u, dec, bt, ct)


def migrate(counts, move_plan, ssm_state, conv_flat):
    owners = lax.axis_size("req")
    slots = ssm_state.shape[0]
    reqs = move_plan.shape[0]
    owner = lax.axis_index("req")
    ids = jnp.arange(reqs, dtype=jnp.int32)
    home = ids // slots
    live = ids % slots < jnp.take(counts, home)
    dest_owner = move_plan // slots
    outgoing = live & (home == owner) & (dest_owner != owner)
    send_j = jnp.sum(jnp.where(outgoing, ids, 0)) % slots
    owner_ids = jnp.arange(owners, dtype=jnp.int32)
    incoming = (
        live[None, :]
        & (dest_owner[None, :] == owner_ids[:, None])
        & (home[None, :] != owner_ids[:, None])
    )
    src_owner = jnp.sum(jnp.where(incoming, ids[None, :], 0), axis=1) // slots
    out_state = lax.dynamic_index_in_dim(ssm_state, send_j, 0, keepdims=False)
    out_conv = lax.dynamic_index_in_dim(conv_flat, send_j, 0, keepdims=False)
    state_words = out_state.reshape(owners, -1)
    conv_words = out_conv.astype(jnp.float32).reshape(owners, -1)
    split = state_words.shape[1]
    packed = jnp.concatenate([state_words, conv_words], 1)
    half = packed.shape[1] // 2
    chunks = [packed[:, :half], packed[:, half:]]
    spreads = [
        lax.all_to_all(c, "req", split_axis=0, concat_axis=0, tiled=True) for c in chunks
    ]
    arrived = jnp.concatenate([
        lax.all_to_all(
            jnp.take(s, src_owner, axis=0), "req", split_axis=0, concat_axis=0, tiled=True
        )
        for s in spreads
    ], 1)
    rstate = arrived[:, :split].reshape((1,) + ssm_state.shape[1:])
    rconv = arrived[:, split:].astype(jnp.bfloat16).reshape(1, -1)
    targets = owner * slots + jnp.arange(slots, dtype=jnp.int32)
    match = live[None, :] & (move_plan[None, :] == targets[:, None])
    hit = jnp.any(match, axis=1)
    source = jnp.sum(jnp.where(match, ids[None, :], 0), axis=1)
    use_recv = hit & (source // slots != owner)
    local = jnp.where(hit & ~use_recv, source % slots, 0)
    sel = jnp.concatenate([local, use_recv.astype(jnp.int32), hit.astype(jnp.int32)])
    conv = jnp.where(use_recv[:, None], rconv, jnp.take(conv_flat, local, axis=0))
    return sel, rstate, conv, hit.astype(jnp.float32)


def on_device(
    counts,
    move_plan,
    ssm_state,
    conv_x_state,
    conv_bc_state,
    x_in,
    bc_in,
    z_in,
    dt_in,
    conv_w_x,
    conv_b_x,
    conv_w_bc,
    conv_b_bc,
    dt_bias,
    a_log,
    d_skip,
    norm_w,
):
    slots, heads_loc, columns = ssm_state.shape
    places, steps, channels = x_in.shape
    groups_loc = conv_bc_state.shape[2]
    pair = conv_bc_state.shape[3]
    state_size = pair // 2
    head_dim = channels // heads_loc
    conv_flat = jnp.concatenate(
        [conv_x_state.reshape(slots, -1), conv_bc_state.reshape(slots, -1)], 1
    )
    sel, recv, conv, mask = migrate(counts, move_plan, ssm_state, conv_flat)
    conv_x = conv[:, : 3 * channels].reshape(places, 3, channels)
    conv_bc = conv[:, 3 * channels :].reshape(places, 3, groups_loc, pair)
    per_group = heads_loc // groups_loc

    seq_x = jnp.concatenate([conv_x, x_in], 1)
    seq_bc = jnp.concatenate([conv_bc, bc_in], 1)
    wx = seq_x.astype(jnp.float32)
    wbc = seq_bc.astype(jnp.float32)
    xconv = conv_b_x + sum(wx[:, k:k + steps] * conv_w_x[k] for k in range(4))
    xconv = jax.nn.silu(xconv)
    bconv = conv_b_bc + sum(wbc[:, k:k + steps] * conv_w_bc[k] for k in range(4))
    bconv = jax.nn.silu(bconv)
    delta = jax.nn.softplus(dt_in + dt_bias)
    decay = jnp.exp(-delta * jnp.exp(a_log))
    heads_x = xconv.reshape(places, steps, heads_loc, head_dim)
    u = delta[..., None] * heads_x
    dec = decay[..., None]
    reps = columns // state_size
    bt = jnp.tile(bconv[..., :state_size], (1, 1, 1, reps)).transpose(0, 2, 1, 3)
    ct = jnp.tile(bconv[..., state_size:], (1, 1, 1, reps)).transpose(0, 2, 1, 3)
    new_state, yk = ssm_steps(sel, ssm_state, recv, u, dec, bt, ct)
    mixed = yk + d_skip[None, None, :, None] * heads_x
    gated = mixed.reshape(places, steps, channels) * jax.nn.silu(z_in.astype(jnp.float32))
    total = lax.psum(jnp.sum(gated * gated, axis=-1), "tp")
    scaling = 1.0 / (H * P_SIZE)
    normed = gated * lax.rsqrt(total * scaling + 1e-05)[..., None] * norm_w
    y_out = (normed * mask[:, None, None]).astype(jnp.bfloat16)
    filled = mask > 0.5
    new_conv_x = jnp.where(filled[:, None, None], seq_x[:, steps:], jnp.zeros((), jnp.bfloat16))
    new_conv_bc = jnp.where(
        filled[:, None, None, None], seq_bc[:, steps:], jnp.zeros((), jnp.bfloat16)
    )
    return (y_out, new_state, new_conv_x, new_conv_bc)


def solution(mesh):
    in_specs = (
        P("parts"),
        P("parts"),
        P(("parts", "req"), "tp", None),
        P(("parts", "req"), None, "tp"),
        P(("parts", "req"), None, "tp", None),
        P(("parts", "req"), None, "tp"),
        P(("parts", "req"), None, "tp", None),
        P(("parts", "req"), None, "tp"),
        P(("parts", "req"), None, "tp"),
        P(None, "tp"),
        P("tp"),
        P(None, "tp", None),
        P("tp", None),
        P("tp"),
        P("tp"),
        P("tp"),
        P("tp"),
    )
    out_specs = (
        P(("parts", "req"), None, "tp"),
        P(("parts", "req"), "tp", None),
        P(("parts", "req"), None, "tp"),
        P(("parts", "req"), None, "tp", None),
    )
    return jax.shard_map(
        on_device, mesh=mesh, in_specs=in_specs, out_specs=out_specs, check_vma=False
    )
```

```python
import jax
import jax.numpy as jnp
from jax import lax
from jax.experimental import pallas as pl
from jax.experimental.pallas import tpu as pltpu
from jax.sharding import PartitionSpec as P

H = 128
P_SIZE = 64
STEPS = 4


def ssm_kernel(sel_ref, s_ref, r_ref, u_ref, dec_ref, b_ref, c_ref, out_ref, y_ref):
    k = pl.program_id(0)
    places = pl.num_programs(0)
    rows, cols = s_ref.shape[1], s_ref.shape[2]
    seg = u_ref.shape[3]
    lane_seg = lax.broadcasted_iota(jnp.int32, (seg, cols), 1) // (cols // seg)
    expand = (lane_seg == lax.broadcasted_iota(jnp.int32, (seg, cols), 0)).astype(jnp.bfloat16)
    nsz = b_ref.shape[3]
    tiler = (
        lax.broadcasted_iota(jnp.int32, (nsz, cols), 1) % nsz
        == lax.broadcasted_iota(jnp.int32, (nsz, cols), 0)
    ).astype(jnp.bfloat16)

    def spread(v):
        v_hi = v.astype(jnp.bfloat16)
        v_lo = (v - v_hi.astype(jnp.float32)).astype(jnp.bfloat16)
        return jnp.dot(v_hi, tiler, preferred_element_type=jnp.float32) + jnp.dot(
            v_lo, tiler, preferred_element_type=jnp.float32
        )

    b_all = spread(b_ref[0, 0])
    c_all = spread(c_ref[0, 0])
    state = jnp.where(sel_ref[places + k] == 1, r_ref[0], s_ref[0])
    for t in range(STEPS):
        u = u_ref[0, t]
        u_hi = u.astype(jnp.bfloat16)
        u_lo = (u - u_hi.astype(jnp.float32)).astype(jnp.bfloat16)
        upd = jnp.dot(u_hi, expand, preferred_element_type=jnp.float32) + jnp.dot(
            u_lo, expand, preferred_element_type=jnp.float32
        )
        state = dec_ref[0, t] * state + upd * b_all[t:t + 1, :]
        prod = state * c_all[t:t + 1, :]
        p_hi = prod.astype(jnp.bfloat16)
        p_lo = (prod - p_hi.astype(jnp.float32)).astype(jnp.bfloat16)
        dims = (((1,), (1,)), ((), ()))
        y_ref[0, t] = lax.dot_general(
            p_hi, expand, dims, preferred_element_type=jnp.float32
        ) + lax.dot_general(p_lo, expand, dims, preferred_element_type=jnp.float32)
    keep = (sel_ref[2 * places + k] == 1).astype(jnp.float32)
    out_ref[0] = state * keep


def ssm_steps(sel, state, recv, u, dec, bt, ct):
    places, heads, cols = state.shape
    groups = bt.shape[1]
    per = heads // groups
    steps = u.shape[1]
    seg = u.shape[3]
    nsz = bt.shape[3]
    grid_spec = pltpu.PrefetchScalarGridSpec(
        num_scalar_prefetch=1,
        grid=(places, groups),
        in_specs=[
            pl.BlockSpec((1, per, cols), lambda k, g, s: (s[k], g, 0)),
            pl.BlockSpec((1, per, cols), lambda k, g, s: (0, g, 0)),
            pl.BlockSpec((1, steps, per, seg), lambda k, g, s: (k, 0, g, 0)),
            pl.BlockSpec((1, steps, per, 1), lambda k, g, s: (k, 0, g, 0)),
            pl.BlockSpec((1, 1, steps, nsz), lambda k, g, s: (k, g, 0, 0)),
            pl.BlockSpec((1, 1, steps, nsz), lambda k, g, s: (k, g, 0, 0)),
        ],
        out_specs=[
            pl.BlockSpec((1, per, cols), lambda k, g, s: (k, g, 0)),
            pl.BlockSpec((1, steps, per, seg), lambda k, g, s: (k, 0, g, 0)),
        ],
    )
    return pl.pallas_call(
        ssm_kernel,
        grid_spec=grid_spec,
        out_shape=[
            jax.ShapeDtypeStruct(state.shape, jnp.float32),
            jax.ShapeDtypeStruct(u.shape, jnp.float32),
        ],
    )(sel, state, recv, u, dec, bt, ct)


def migrate(counts, move_plan, ssm_state, conv_flat):
    owners = lax.axis_size("req")
    slots = ssm_state.shape[0]
    reqs = move_plan.shape[0]
    owner = lax.axis_index("req")
    ids = jnp.arange(reqs, dtype=jnp.int32)
    home = ids // slots
    live = ids % slots < jnp.take(counts, home)
    dest_owner = move_plan // slots
    outgoing = live & (home == owner) & (dest_owner != owner)
    send_j = jnp.sum(jnp.where(outgoing, ids, 0)) % slots
    owner_ids = jnp.arange(owners, dtype=jnp.int32)
    incoming = (
        live[None, :]
        & (dest_owner[None, :] == owner_ids[:, None])
        & (home[None, :] != owner_ids[:, None])
    )
    src_owner = jnp.sum(jnp.where(incoming, ids[None, :], 0), axis=1) // slots
    out_state = lax.dynamic_index_in_dim(ssm_state, send_j, 0, keepdims=False)
    out_conv = lax.dynamic_index_in_dim(conv_flat, send_j, 0, keepdims=False)
    state_words = out_state.reshape(owners, -1)
    conv_words = out_conv.astype(jnp.float32).reshape(owners, -1)
    split = state_words.shape[1]
    packed = jnp.concatenate([state_words, conv_words], 1)
    spread = lax.all_to_all(packed, "req", split_axis=0, concat_axis=0, tiled=True)
    picked = jnp.take(spread, src_owner, axis=0)
    arrived = lax.all_to_all(picked, "req", split_axis=0, concat_axis=0, tiled=True)
    rstate = arrived[:, :split].reshape((1,) + ssm_state.shape[1:])
    rconv = arrived[:, split:].astype(jnp.bfloat16).reshape(1, -1)
    targets = owner * slots + jnp.arange(slots, dtype=jnp.int32)
    match = live[None, :] & (move_plan[None, :] == targets[:, None])
    hit = jnp.any(match, axis=1)
    source = jnp.sum(jnp.where(match, ids[None, :], 0), axis=1)
    use_recv = hit & (source // slots != owner)
    local = jnp.where(hit & ~use_recv, source % slots, 0)
    sel = jnp.concatenate([local, use_recv.astype(jnp.int32), hit.astype(jnp.int32)])
    conv = jnp.where(use_recv[:, None], rconv, jnp.take(conv_flat, local, axis=0))
    return sel, rstate, conv, hit.astype(jnp.float32)


def on_device(
    counts,
    move_plan,
    ssm_state,
    conv_x_state,
    conv_bc_state,
    x_in,
    bc_in,
    z_in,
    dt_in,
    conv_w_x,
    conv_b_x,
    conv_w_bc,
    conv_b_bc,
    dt_bias,
    a_log,
    d_skip,
    norm_w,
):
    slots, heads_loc, columns = ssm_state.shape
    places, steps, channels = x_in.shape
    groups_loc = conv_bc_state.shape[2]
    pair = conv_bc_state.shape[3]
    state_size = pair // 2
    head_dim = channels // heads_loc
    conv_flat = jnp.concatenate(
        [conv_x_state.reshape(slots, -1), conv_bc_state.reshape(slots, -1)], 1
    )
    sel, recv, conv, mask = migrate(counts, move_plan, ssm_state, conv_flat)
    conv_x = conv[:, : 3 * channels].reshape(places, 3, channels)
    conv_bc = conv[:, 3 * channels :].reshape(places, 3, groups_loc, pair)
    per_group = heads_loc // groups_loc

    seq_x = jnp.concatenate([conv_x, x_in], 1)
    seq_bc = jnp.concatenate([conv_bc, bc_in], 1)
    wx = seq_x.astype(jnp.float32)
    wbc = seq_bc.astype(jnp.float32)
    xconv = conv_b_x + sum(wx[:, k:k + steps] * conv_w_x[k] for k in range(4))
    xconv = jax.nn.silu(xconv)
    bconv = conv_b_bc + sum(wbc[:, k:k + steps] * conv_w_bc[k] for k in range(4))
    bconv = jax.nn.silu(bconv)
    delta = jax.nn.softplus(dt_in + dt_bias)
    decay = jnp.exp(-delta * jnp.exp(a_log))
    heads_x = xconv.reshape(places, steps, heads_loc, head_dim)
    u = delta[..., None] * heads_x
    dec = decay[..., None]
    bt = bconv[..., :state_size].transpose(0, 2, 1, 3)
    ct = bconv[..., state_size:].transpose(0, 2, 1, 3)
    new_state, yk = ssm_steps(sel, ssm_state, recv, u, dec, bt, ct)
    mixed = yk + d_skip[None, None, :, None] * heads_x
    gated = mixed.reshape(places, steps, channels) * jax.nn.silu(z_in.astype(jnp.float32))
    total = lax.psum(jnp.sum(gated * gated, axis=-1), "tp")
    scaling = 1.0 / (H * P_SIZE)
    normed = gated * lax.rsqrt(total * scaling + 1e-05)[..., None] * norm_w
    y_out = (normed * mask[:, None, None]).astype(jnp.bfloat16)
    filled = mask > 0.5
    new_conv_x = jnp.where(filled[:, None, None], seq_x[:, steps:], jnp.zeros((), jnp.bfloat16))
    new_conv_bc = jnp.where(
        filled[:, None, None, None], seq_bc[:, steps:], jnp.zeros((), jnp.bfloat16)
    )
    return (y_out, new_state, new_conv_x, new_conv_bc)


def solution(mesh):
    in_specs = (
        P("parts"),
        P("parts"),
        P(("parts", "req"), "tp", None),
        P(("parts", "req"), None, "tp"),
        P(("parts", "req"), None, "tp", None),
        P(("parts", "req"), None, "tp"),
        P(("parts", "req"), None, "tp", None),
        P(("parts", "req"), None, "tp"),
        P(("parts", "req"), None, "tp"),
        P(None, "tp"),
        P("tp"),
        P(None, "tp", None),
        P("tp", None),
        P("tp"),
        P("tp"),
        P("tp"),
        P("tp"),
    )
    out_specs = (
        P(("parts", "req"), None, "tp"),
        P(("parts", "req"), "tp", None),
        P(("parts", "req"), None, "tp"),
        P(("parts", "req"), None, "tp", None),
    )
    return jax.shard_map(
        on_device, mesh=mesh, in_specs=in_specs, out_specs=out_specs, check_vma=False
    )
```
